32 devices in a mesh: replica: 4 (over y, core), shard: 8 (over z, x).
Axes of the slice: x: 2, y: 2, z: 4, core: 2. Of those that a mesh axis runs over, the one named last changes fastest.
Arguments:
- enc_delta: bfloat16 [4, 5120, 8192], P('replica', 'shard'), may hold values from -6 to 6
- enc_params: float32 [4, 8, 160, 8192], P('replica', 'shard'), may hold values from -6 to 6
- enc_momentum: float32 [4, 8, 160, 8192], P('replica', 'shard'), may hold values from -6 to 6
- dec_delta: bfloat16 [4, 5120, 8192], P('replica', 'shard'), may hold values from -6 to 6
- dec_params: float32 [4, 8, 160, 8192], P('replica', 'shard'), may hold values from -6 to 6
- dec_momentum: float32 [4, 8, 160, 8192], P('replica', 'shard'), may hold values from -6 to 6
Outputs:
- enc_params_new: float32 [4, 8, 160, 8192], P('replica', 'shard')
- enc_momentum_new: float32 [4, 8, 160, 8192], P('replica', 'shard')
- enc_working: bfloat16 [5120, 8192], P('shard')
- dec_params_new: float32 [4, 8, 160, 8192], P('replica', 'shard')
- dec_momentum_new: float32 [4, 8, 160, 8192], P('replica', 'shard')
- dec_working: bfloat16 [5120, 8192], P('shard')
The draws below stay inside these ranges and needn't reach their ends.
All inputs are finite; a program needn't handle non-finite values.
Results may differ from the reference program's by a relative error of at most 0.007.
Values may be sent and summed in bfloat16 or wider, within the bound.
No kernel may reach another device: no remote copies, remote signals or barrier semaphores. Data moves between devices by JAX's collectives and lax.ppermute only.
A program may use at most 192 MiB of HBM per device.

```python
import jax
import jax.numpy as jnp

D = 4096
FFW = 5120
SLAB = 160
N_REPLICA = 4
N_SHARD = 8


def steps_of(rng, extent, split, least, high):
    loudness = 1.0
    for position, blocks in split:
        draws = jax.random.uniform(jax.random.fold_in(jax.random.fold_in(rng, 6), position), (blocks,), jnp.float32, least / len(split), high / len(split))
        loudness = loudness * jnp.repeat(jnp.exp(draws), extent[position] // blocks).reshape((-1,) + (1,) * (len(extent) - 1 - position))
    return loudness


def scatter_about(key, extent, deviation, reach, split=(), dtype=jnp.bfloat16):
    values = deviation * jax.random.normal(key, extent, jnp.float32)
    if split:
        values = values * steps_of(key, extent, split, -0.22, 0.18)
    return jnp.clip(values, -reach, reach).astype(dtype)


def setup_inputs(seed: int = 0) -> dict:
    seeds = jax.random.split(jax.random.key(seed), 7)
    enc_delta = scatter_about(seeds[0], (N_REPLICA, FFW, 2 * D), 1.0, 6.0, ((0, 4), (1, 8)))
    enc_params = scatter_about(seeds[1], (N_REPLICA, N_SHARD, SLAB, 2 * D), 1.0, 6.0, ((0, 4), (1, 8)), jnp.float32)
    enc_momentum = scatter_about(seeds[2], (N_REPLICA, N_SHARD, SLAB, 2 * D), 1.0, 6.0, ((0, 4), (1, 8)), jnp.float32)
    dec_delta = scatter_about(seeds[3], (N_REPLICA, FFW, 2 * D), 1.0, 6.0, ((0, 4), (1, 8)))
    dec_params = scatter_about(seeds[4], (N_REPLICA, N_SHARD, SLAB, 2 * D), 1.0, 6.0, ((0, 4), (1, 8)), jnp.float32)
    dec_momentum = scatter_about(seeds[5], (N_REPLICA, N_SHARD, SLAB, 2 * D), 1.0, 6.0, ((0, 4), (1, 8)), jnp.float32)
    return dict(enc_delta=enc_delta, enc_params=enc_params, enc_momentum=enc_momentum, dec_delta=dec_delta, dec_params=dec_params, dec_momentum=dec_momentum)


outer_rate = 0.7
nesterov_keep = 0.9


def outer_block(deltas, params, momentum):
    rows_dev = FFW // N_SHARD
    slab_rows = rows_dev // N_REPLICA
    summed = jnp.sum(deltas.astype(jnp.float32), axis=0)
    average = summed / N_REPLICA
    owned_grad = average.reshape(N_SHARD, N_REPLICA, slab_rows, 2 * D).transpose(1, 0, 2, 3)
    momentum_new = nesterov_keep * momentum + owned_grad
    params_new = params - outer_rate * (owned_grad + nesterov_keep * momentum_new)
    working = params_new.astype(jnp.bfloat16).transpose(1, 0, 2, 3).reshape(FFW, 2 * D)
    return params_new, momentum_new, working


def reference(enc_delta, enc_params, enc_momentum, dec_delta, dec_params, dec_momentum):
    encoder_out = outer_block(enc_delta, enc_params, enc_momentum)
    decoder_out = outer_block(dec_delta, dec_params, dec_momentum)
    return (encoder_out[0], encoder_out[1], encoder_out[2], decoder_out[0], decoder_out[1], decoder_out[2])
```

```python
import functools

import jax
import jax.numpy as jnp
from jax import lax
from jax.experimental import pallas as pl
from jax.experimental.pallas import tpu as pltpu
from jax.sharding import PartitionSpec as P


outer_rate = 0.7
nesterov_keep = 0.9
lane = 128
widest = 8
vmem_bytes = 67_043_328

first_shares = (4, 4, 8, 16, 32)
last_shares = (32, 16, 8, 4, 4)

f32 = jnp.float32
bf16 = jnp.bfloat16


def chunks_of(columns, shares):
    units = columns // lane
    total = sum(shares)
    edges, seen = [0], 0
    for share in shares:
        seen += share
        edges.append(max(edges[-1], units * seen // total))
    return [(a, b - a) for a, b in zip(edges[:-1], edges[1:]) if b > a]


def step_of(start, width):
    for units in (widest, 4, 2, 1):
        if start % units == 0 and width % units == 0:
            return units
    return 1


def me():
    return lax.axis_index("replica")


def near_of(r):
    return r + 1 - 2 * lax.rem(r, 2)


def far_of(r):
    half = lax.axis_size("replica") // 2
    return lax.rem(r + half, 2 * half)


def slab_spec(rows, step, start, which):
    return pl.BlockSpec(
        (1, rows, step * lane),
        lambda i: (which(me()), 0, start // step + i),
    )


def state_spec(rows, step, start):
    return pl.BlockSpec((rows, step * lane), lambda i: (0, start // step + i))


def pair_spec(rows, step):
    return pl.BlockSpec((2, rows, step * lane), lambda i: (0, 0, i))


def same(r):
    return r


def near_far(r):
    return far_of(near_of(r))


def estimate(bytes_moved):
    return pl.CostEstimate(
        flops=bytes_moved, bytes_accessed=bytes_moved, transcendentals=0
    )


def compiler_params():
    return pltpu.CompilerParams(vmem_limit_bytes=vmem_bytes)


def pick_kernel(one_ref, two_ref, *refs):
    out_ref = refs[-1]
    out_ref[0] = one_ref[0]
    out_ref[1] = two_ref[0]


def pick(delta, start, width, after):
    _, rows, _ = delta.shape
    step = step_of(start, width)
    return pl.pallas_call(
        pick_kernel,
        grid=(width // step,),
        in_specs=[
            slab_spec(rows, step, start, near_of),
            slab_spec(rows, step, start, near_far),
        ]
        + [pl.BlockSpec(memory_space=pl.ANY)] * len(after),
        out_specs=pair_spec(rows, step),
        out_shape=pltpu.HBM((2, rows, width * lane), bf16),
        cost_estimate=estimate(8 * rows * width * lane),
        compiler_params=compiler_params(),
        name="pick",
    )(delta, delta, *after)


def share(replicas):
    return outer_rate * (1 + nesterov_keep) / replicas


def send_kernel(
    replicas, own_ref, away_ref, got_ref, params_ref, momentum_ref, out_ref
):
    out_ref[0] = (away_ref[0].astype(f32) + got_ref[1].astype(f32)).astype(bf16)
    summed = own_ref[0].astype(f32) + got_ref[0].astype(f32)
    base = params_ref[...] - (outer_rate * nesterov_keep**2) * momentum_ref[...]
    out_ref[1] = (base - share(replicas) * summed).astype(bf16)


def send_part(replicas, delta, got, params, momentum, start, width):
    _, rows, _ = delta.shape
    step = step_of(start, width)
    return pl.pallas_call(
        functools.partial(send_kernel, replicas),
        grid=(width // step,),
        in_specs=[
            slab_spec(rows, step, start, same),
            slab_spec(rows, step, start, far_of),
            pair_spec(rows, step),
            state_spec(rows, step, start),
            state_spec(rows, step, start),
        ],
        out_specs=pair_spec(rows, step),
        out_shape=pltpu.HBM((2, rows, width * lane), bf16),
        cost_estimate=estimate(20 * rows * width * lane),
        compiler_params=compiler_params(),
        name="send_part",
    )(delta, delta, got, params, momentum)


def finish_kernel(
    replicas,
    own_ref,
    got_ref,
    sent_ref,
    far_ref,
    near_sent_ref,
    near_far_ref,
    params_ref,
    momentum_ref,
    *refs,
):
    params_new_ref, momentum_new_ref, working_ref = refs[-3:]
    r = me()
    k = share(replicas)

    def joined(base, summed):
        return (base.astype(f32) - k * summed.astype(f32)).astype(bf16)

    summed = own_ref[0].astype(f32) + got_ref[0].astype(f32)
    average = (summed + far_ref[0].astype(f32)) * (1 / replicas)
    momentum_new = nesterov_keep * momentum_ref[...] + average
    momentum_new_ref[...] = momentum_new
    params_new_ref[...] = params_ref[...] - outer_rate * (
        average + nesterov_keep * momentum_new
    )
    working_ref[r] = joined(sent_ref[1], far_ref[0])
    working_ref[far_of(r)] = joined(far_ref[1], sent_ref[0])
    working_ref[near_of(r)] = joined(near_sent_ref[1], near_far_ref[0])
    working_ref[near_far(r)] = joined(near_far_ref[1], near_sent_ref[0])


def finish(
    replicas, delta, got, sent, far, near_sent, near_far_got, params, momentum,
    start, width, results, after,
):
    _, rows, columns = delta.shape
    step = step_of(start, width)
    out_shape = (
        jax.ShapeDtypeStruct((rows, columns), f32),
        jax.ShapeDtypeStruct((rows, columns), f32),
        jax.ShapeDtypeStruct((replicas, rows, columns), bf16),
    )
    operands = [delta, got, sent, far, near_sent, near_far_got, params, momentum]
    pair = pair_spec(rows, step)
    in_specs = [
        slab_spec(rows, step, start, same), pair, pair, pair, pair, pair,
        state_spec(rows, step, start), state_spec(rows, step, start),
    ]
    aliases = {}
    for array in after:
        operands.append(array)
        in_specs.append(pl.BlockSpec(memory_space=pl.ANY))
    if results is not None:
        for i, array in enumerate(results):
            aliases[len(operands)] = i
            operands.append(array)
            in_specs.append(pl.BlockSpec(memory_space=pl.ANY))
    return pl.pallas_call(
        functools.partial(finish_kernel, replicas),
        grid=(width // step,),
        in_specs=in_specs,
        out_specs=(
            state_spec(rows, step, start),
            state_spec(rows, step, start),
            pl.BlockSpec(
                (replicas, rows, step * lane), lambda i: (0, 0, start // step + i)
            ),
        ),
        out_shape=out_shape,
        input_output_aliases=aliases,
        cost_estimate=estimate(44 * rows * width * lane),
        compiler_params=compiler_params(),
        name="finish",
    )(*operands)


def local(enc_delta, enc_params, enc_momentum, dec_delta, dec_params, dec_momentum):
    replicas = lax.axis_size("replica")
    near = [(r, r + 1 - 2 * (r % 2)) for r in range(replicas)]
    far = [(r, (r + replicas // 2) % replicas) for r in range(replicas)]

    def swap(x, pairs):
        return lax.ppermute(x, "replica", pairs)

    parts = []
    for block, (deltas, params, momentum, shares) in enumerate((
        (enc_delta, enc_params, enc_momentum, first_shares),
        (dec_delta, dec_params, dec_momentum, last_shares),
    )):
        _, _, rows, columns = params.shape
        delta = deltas.reshape(replicas, rows, columns)
        params = params.reshape(rows, columns)
        momentum = momentum.reshape(rows, columns)
        for start, width in chunks_of(columns, shares):
            parts.append((block, delta, params, momentum, start, width))

    gots, sents, cames, near_sents = [], [], [], []
    for i, (_, delta, params, momentum, start, width) in enumerate(parts):
        picked = pick(delta, start, width, sents[i - 2 : i - 1] if i > 1 else [])
        got = swap(picked, near)
        sent = send_part(replicas, delta, got, params, momentum, start, width)
        came = swap(sent, far)
        near_sent = swap(sent, near)
        gots.append(got)
        sents.append(sent)
        cames.append(came)
        near_sents.append(near_sent)

    arrays = [None, None]
    after = sents[-1:]
    for i, (block, delta, params, momentum, start, width) in enumerate(parts):
        near_came = swap(cames[i], near)
        arrays[block] = finish(
            replicas, delta, gots[i], sents[i], cames[i], near_sents[i], near_came,
            params, momentum, start, width, arrays[block], after,
        )
        after = []

    results = []
    for params_new, momentum_new, working in arrays:
        rows, columns = params_new.shape
        results.append(
            (
                params_new.reshape(1, 1, rows, columns),
                momentum_new.reshape(1, 1, rows, columns),
                working.reshape(replicas * rows, columns),
            )
        )
    return (*results[0], *results[1])


def solution(mesh):
    delta_spec = P("replica", "shard", None)
    state = P("replica", "shard", None, None)
    return jax.shard_map(
        local,
        mesh=mesh,
        in_specs=(delta_spec, state, state, delta_spec, state, state),
        out_specs=(state, state, P("shard", None), state, state, P("shard", None)),
        check_vma=False,
    )
```

```python
import functools

import jax
import jax.numpy as jnp
from jax import lax
from jax.experimental import pallas as pl
from jax.experimental.pallas import tpu as pltpu
from jax.sharding import PartitionSpec as P


outer_rate = 0.7
nesterov_keep = 0.9
lane = 128
widest = 8
vmem_bytes = 67_043_328

first_shares = (4, 2, 2, 8, 16, 32)
raw_share = 1
last_shares = (32, 16, 8, 4, 4)

f32 = jnp.float32
bf16 = jnp.bfloat16


def chunks_of(columns, shares):
    units = columns // lane
    total = sum(shares)
    edges, seen = [0], 0
    for share in shares:
        seen += share
        edges.append(max(edges[-1], units * seen // total))
    return [(a, b - a) for a, b in zip(edges[:-1], edges[1:]) if b > a]


def step_of(start, width):
    for units in (widest, 4, 2, 1):
        if start % units == 0 and width % units == 0:
            return units
    return 1


def cores():
    return lax.axis_size("replica") // 2


def chip_core():
    r = lax.axis_index("replica")
    return r // cores(), lax.rem(r, cores())


def other(i):
    return 1 - i


def slab(far, near):
    chip, core = chip_core()
    return (other(chip) if far else chip), (other(core) if near else core)


def slab_spec(rows, step, start, far, near):
    return pl.BlockSpec(
        (1, 1, rows, step * lane),
        lambda i: (*slab(far, near), 0, start // step + i),
    )


def got_spec(rows, step, far):
    return pl.BlockSpec(
        (1, rows, step * lane), lambda i: (slab(far, False)[0], 0, i)
    )


def state_spec(rows, step, start):
    return pl.BlockSpec((rows, step * lane), lambda i: (0, start // step + i))


def half_spec(rows, step, half):
    return pl.BlockSpec((1, rows, step * lane), lambda i: (half, 0, i))


def any_spec():
    return pl.BlockSpec(memory_space=pl.ANY)


def estimate(bytes_moved):
    return pl.CostEstimate(
        flops=bytes_moved, bytes_accessed=bytes_moved, transcendentals=0
    )


def compiler_params(limit=vmem_bytes):
    return pltpu.CompilerParams(vmem_limit_bytes=limit)


def share(replicas):
    return outer_rate * (1 + nesterov_keep) / replicas


def based(replicas, params, momentum, summed):
    kept = params - (outer_rate * nesterov_keep**2) * momentum
    return (kept - share(replicas) * summed).astype(bf16)


def joined(replicas, base, summed):
    return (base.astype(f32) - share(replicas) * summed.astype(f32)).astype(bf16)


def pick_kernel(in_ref, *refs):
    refs[-1][...] = in_ref[:, 0]


def pick(delta, start, width, after):
    chips, _, rows, _ = delta.shape
    step = step_of(start, width)
    return pl.pallas_call(
        pick_kernel,
        grid=(width // step,),
        in_specs=[
            pl.BlockSpec(
                (chips, 1, rows, step * lane),
                lambda i: (0, slab(False, True)[1], 0, start // step + i),
            )
        ]
        + [any_spec()] * len(after),
        out_specs=pl.BlockSpec((chips, rows, step * lane), lambda i: (0, 0, i)),
        out_shape=pltpu.HBM((chips, rows, width * lane), bf16),
        cost_estimate=estimate(8 * rows * width * lane),
        compiler_params=compiler_params(),
        name="pick",
    )(delta, *after)


def open_kernel(near_ref, far_ref, picked_ref, raw_ref):
    picked_ref[...] = near_ref[:, 0]
    raw_ref[...] = far_ref[0]


def open_part(delta, start, width, raw_start, raw_width):
    chips, cores_, rows, _ = delta.shape
    return pl.pallas_call(
        open_kernel,
        grid=(1,),
        in_specs=[
            pl.BlockSpec(
                (chips, 1, rows, width * lane),
                lambda i: (0, slab(False, True)[1], 0, start // width),
            ),
            pl.BlockSpec(
                (1, cores_, rows, raw_width * lane),
                lambda i: (slab(True, False)[0], 0, 0, raw_start // raw_width),
            ),
        ],
        out_specs=(
            pl.BlockSpec((chips, rows, width * lane), lambda i: (0, 0, 0)),
            pl.BlockSpec((cores_, rows, raw_width * lane), lambda i: (0, 0, 0)),
        ),
        out_shape=(
            pltpu.HBM((chips, rows, width * lane), bf16),
            pltpu.HBM((cores_, rows, raw_width * lane), bf16),
        ),
        cost_estimate=estimate(8 * rows * (width + raw_width) * lane),
        compiler_params=compiler_params(),
        name="open_part",
    )(delta, delta)


def merge_kernel(raw_ref, near_raw_ref, base_ref, near_base_ref, far_ref, near_ref):
    core = slab(False, False)[1]
    for out_ref, which, base in (
        (far_ref, core, base_ref),
        (near_ref, other(core), near_base_ref),
    ):
        out_ref[0] = (
            raw_ref[which].astype(f32) + near_raw_ref[which].astype(f32)
        ).astype(bf16)
        out_ref[1] = base[0]


def merge(raw, near_raw, base, near_base):
    shape = pltpu.HBM(raw.shape, bf16)
    return pl.pallas_call(
        merge_kernel,
        out_shape=(shape, shape),
        cost_estimate=estimate(10 * base.size),
        compiler_params=compiler_params(),
        name="merge",
    )(raw, near_raw, base, near_base)


def send_kernel(
    replicas, own_ref, away_ref, got_ref, got_away_ref, params_ref, momentum_ref, out_ref
):
    out_ref[0] = (away_ref[0, 0].astype(f32) + got_away_ref[0].astype(f32)).astype(bf16)
    summed = own_ref[0, 0].astype(f32) + got_ref[0].astype(f32)
    out_ref[1] = based(replicas, params_ref[...], momentum_ref[...], summed)


def send_part(replicas, delta, got, params, momentum, start, width, limit):
    _, _, rows, _ = delta.shape
    step = step_of(start, width)
    return pl.pallas_call(
        functools.partial(send_kernel, replicas),
        grid=(width // step,),
        in_specs=[
            slab_spec(rows, step, start, False, False),
            slab_spec(rows, step, start, True, False),
            got_spec(rows, step, False),
            got_spec(rows, step, True),
            state_spec(rows, step, start),
            state_spec(rows, step, start),
        ],
        out_specs=pl.BlockSpec((2, rows, step * lane), lambda i: (0, 0, i)),
        out_shape=pltpu.HBM((2, rows, width * lane), bf16),
        cost_estimate=estimate(20 * rows * width * lane),
        compiler_params=compiler_params(limit),
        name="send_part",
    )(delta, delta, got, got, params, momentum)


def finish_kernel(replicas, own, near, *refs):
    outs = refs[-(2 * own + 1) :]
    working_ref = outs[-1]
    if own:
        (
            own_ref, got_ref, params_ref, momentum_ref,
            sent_sum, sent_base, far_sum, far_base,
        ) = refs[:8]
        refs = refs[8:]
        summed = own_ref[0, 0].astype(f32) + got_ref[0].astype(f32)
        average = (summed + far_sum[0].astype(f32)) * (1 / replicas)
        momentum_new = nesterov_keep * momentum_ref[...] + average
        outs[1][...] = momentum_new
        outs[0][...] = params_ref[...] - outer_rate * (
            average + nesterov_keep * momentum_new
        )
        working_ref[slab(False, False)] = joined(replicas, sent_base[0], far_sum[0])
        working_ref[slab(True, False)] = joined(replicas, far_base[0], sent_sum[0])
    if near:
        sent_sum, sent_base, far_sum, far_base = refs[:4]
        chip, core = slab(False, True) if own else (slab(False, False)[0], 0)
        working_ref[chip, core] = joined(replicas, sent_base[0], far_sum[0])
        working_ref[other(chip), core] = joined(replicas, far_base[0], sent_sum[0])


def finish(replicas, part, got, sent, far, near_sent, near_far, results, after, own, near):
    delta, params, momentum, start, width = part
    chips, cores_, rows, columns = delta.shape
    step = step_of(start, width)
    state = state_spec(rows, step, start)
    state_shape = jax.ShapeDtypeStruct((rows, columns), f32)
    operands, in_specs = [], []
    if own:
        operands += [delta, got, params, momentum]
        in_specs += [
            slab_spec(rows, step, start, False, False),
            got_spec(rows, step, False),
            state,
            state,
        ]
    for wanted, pair in ((own, sent), (own, far), (near, near_sent), (near, near_far)):
        if wanted:
            operands += [pair, pair]
            in_specs += [half_spec(rows, step, 0), half_spec(rows, step, 1)]
    for array in after:
        operands.append(array)
        in_specs.append(any_spec())
    aliases = {}
    if results is not None:
        for i, array in enumerate(results if own else results[-1:]):
            aliases[len(operands)] = i
            operands.append(array)
            in_specs.append(any_spec())
    count = cores_ if own else 1
    working_spec = pl.BlockSpec(
        (chips, count, rows, step * lane),
        lambda i: (0, 0 if own else slab(False, True)[1], 0, start // step + i),
    )
    working_shape = jax.ShapeDtypeStruct(delta.shape, bf16)
    outs = pl.pallas_call(
        functools.partial(finish_kernel, replicas, own, near),
        grid=(width // step,),
        in_specs=in_specs,
        out_specs=(state, state, working_spec) if own else (working_spec,),
        out_shape=(state_shape, state_shape, working_shape) if own else (working_shape,),
        input_output_aliases=aliases,
        cost_estimate=estimate((32 * own + 12 * near) * rows * width * lane),
        compiler_params=compiler_params(),
        name="finish",
    )(*operands)
    return tuple(outs) if own else (*results[:-1], outs[0])


def local(enc_delta, enc_params, enc_momentum, dec_delta, dec_params, dec_momentum):
    replicas = lax.axis_size("replica")
    near = [(r, r + 1 - 2 * (r % 2)) for r in range(replicas)]
    far = [(r, (r + replicas // 2) % replicas) for r in range(replicas)]

    def swap(x, pairs):
        return lax.ppermute(x, "replica", pairs)

    parts = []
    for block, (deltas, params, momentum, shares) in enumerate((
        (enc_delta, enc_params, enc_momentum, first_shares),
        (dec_delta, dec_params, dec_momentum, last_shares),
    )):
        _, _, rows, columns = params.shape
        delta = deltas.reshape(2, replicas // 2, rows, columns)
        params = params.reshape(rows, columns)
        momentum = momentum.reshape(rows, columns)
        chunks = chunks_of(columns, shares)
        if block == 0:
            chunks.append(chunks.pop(raw_share))
        for start, width in chunks:
            parts.append((block, (delta, params, momentum, start, width)))

    raw_at = len(first_shares) - 1
    raw_part = parts[raw_at][1]
    gots, sents, fars, near_sents = [], [], [], []
    for i, (_, part) in enumerate(parts):
        delta, params, momentum, start, width = part
        if i == 0:
            picked, raw = open_part(delta, start, width, *raw_part[3:])
        else:
            behind = [picked] if i == 2 else [sents[i - 1]]
            picked = pick(delta, start, width, behind)
        got = swap(picked, near)
        if i == 0:
            far_raw = swap(raw, far)
        sent = send_part(replicas, delta, got, params, momentum, start, width, vmem_bytes)
        out = sent
        if i == raw_at:
            out = sent[1:]
        came = swap(out, far)
        near_sent = swap(sent, near)
        gots.append(got)
        sents.append(sent)
        fars.append(came)
        near_sents.append(near_sent)

    arrays = [None, None]
    after = [sents[-1]]
    for i, (block, part) in enumerate(parts):
        came = fars[i]
        near_came = swap(came, near)
        if i == raw_at:
            near_raw = swap(far_raw, near)
            came, near_came = merge(far_raw, near_raw, came, near_came)
        last = i == len(parts) - 1
        inputs = (gots[i], sents[i], came, near_sents[i], near_came)
        arrays[block] = finish(
            replicas, part, *inputs, arrays[block], after, True, not last
        )
        if last:
            arrays[block] = finish(
                replicas, part, *inputs, arrays[block], [], False, True
            )
        after = []

    results = []
    for params_new, momentum_new, working in arrays:
        rows, columns = params_new.shape
        results.append(
            (
                params_new.reshape(1, 1, rows, columns),
                momentum_new.reshape(1, 1, rows, columns),
                working.reshape(replicas * rows, columns),
            )
        )
    return (*results[0], *results[1])


def solution(mesh):
    delta_spec = P("replica", "shard", None)
    state = P("replica", "shard", None, None)
    return jax.shard_map(
        local,
        mesh=mesh,
        in_specs=(delta_spec, state, state, delta_spec, state, state),
        out_specs=(state, state, P("shard", None), state, state, P("shard", None)),
        check_vma=False,
    )
```

```python
import functools

import jax
import jax.numpy as jnp
from jax import lax
from jax.experimental import pallas as pl
from jax.experimental.pallas import tpu as pltpu
from jax.sharding import PartitionSpec as P


outer_rate = 0.7
nesterov_keep = 0.9
lane = 128
widest = 8
vmem_bytes = 67_043_328

first_shares = (4, 2, 2, 8, 16, 32)
raw_share = 1
last_shares = (32, 16, 8, 4, 4)

f32 = jnp.float32
bf16 = jnp.bfloat16


def chunks_of(columns, shares):
    units = columns // lane
    total = sum(shares)
    edges, seen = [0], 0
    for share in shares:
        seen += share
        edges.append(max(edges[-1], units * seen // total))
    return [(a, b - a) for a, b in zip(edges[:-1], edges[1:]) if b > a]


def step_of(start, width):
    for units in (widest, 4, 2, 1):
        if start % units == 0 and width % units == 0:
            return units
    return 1


def cores():
    return lax.axis_size("replica") // 2


def chip_core():
    r = lax.axis_index("replica")
    return r // cores(), lax.rem(r, cores())


def other(i):
    return 1 - i


def slab(far, near):
    chip, core = chip_core()
    return (other(chip) if far else chip), (other(core) if near else core)


def slab_spec(rows, step, start, far, near):
    return pl.BlockSpec(
        (1, 1, rows, step * lane),
        lambda i: (*slab(far, near), 0, start // step + i),
    )


def got_spec(rows, step, far):
    return pl.BlockSpec(
        (1, rows, step * lane), lambda i: (slab(far, False)[0], 0, i)
    )


def state_spec(rows, step, start):
    return pl.BlockSpec((rows, step * lane), lambda i: (0, start // step + i))


def half_spec(rows, step, half):
    return pl.BlockSpec((1, rows, step * lane), lambda i: (half, 0, i))


def any_spec():
    return pl.BlockSpec(memory_space=pl.ANY)


def estimate(bytes_moved):
    return pl.CostEstimate(
        flops=bytes_moved, bytes_accessed=bytes_moved, transcendentals=0
    )


def compiler_params():
    return pltpu.CompilerParams(vmem_limit_bytes=vmem_bytes)


def share(replicas):
    return outer_rate * (1 + nesterov_keep) / replicas


def based(replicas, params, momentum, summed):
    kept = params - (outer_rate * nesterov_keep**2) * momentum
    return (kept - share(replicas) * summed).astype(bf16)


def joined(replicas, base, summed):
    return (base.astype(f32) - share(replicas) * summed.astype(f32)).astype(bf16)


def pick_kernel(in_ref, *refs):
    refs[-1][...] = in_ref[:, 0]


def pick(delta, start, width, after):
    chips, _, rows, _ = delta.shape
    step = step_of(start, width)
    return pl.pallas_call(
        pick_kernel,
        grid=(width // step,),
        in_specs=[
            pl.BlockSpec(
                (chips, 1, rows, step * lane),
                lambda i: (0, slab(False, True)[1], 0, start // step + i),
            )
        ]
        + [any_spec()] * len(after),
        out_specs=pl.BlockSpec((chips, rows, step * lane), lambda i: (0, 0, i)),
        out_shape=pltpu.HBM((chips, rows, width * lane), bf16),
        cost_estimate=estimate(8 * rows * width * lane),
        compiler_params=compiler_params(),
        name="pick",
    )(delta, *after)


def open_kernel(near_ref, far_ref, picked_ref, raw_ref):
    picked_ref[...] = near_ref[:, 0]
    raw_ref[...] = far_ref[0]


def open_part(delta, start, width, raw_start, raw_width):
    chips, cores_, rows, _ = delta.shape
    return pl.pallas_call(
        open_kernel,
        grid=(1,),
        in_specs=[
            pl.BlockSpec(
                (chips, 1, rows, width * lane),
                lambda i: (0, slab(False, True)[1], 0, start // width),
            ),
            pl.BlockSpec(
                (1, cores_, rows, raw_width * lane),
                lambda i: (slab(True, False)[0], 0, 0, raw_start // raw_width),
            ),
        ],
        out_specs=(
            pl.BlockSpec((chips, rows, width * lane), lambda i: (0, 0, 0)),
            pl.BlockSpec((cores_, rows, raw_width * lane), lambda i: (0, 0, 0)),
        ),
        out_shape=(
            pltpu.HBM((chips, rows, width * lane), bf16),
            pltpu.HBM((cores_, rows, raw_width * lane), bf16),
        ),
        cost_estimate=estimate(8 * rows * (width + raw_width) * lane),
        compiler_params=compiler_params(),
        name="open_part",
    )(delta, delta)


def merge_kernel(raw_ref, near_raw_ref, base_ref, near_base_ref, far_ref, near_ref):
    core = slab(False, False)[1]
    for out_ref, which, base in (
        (far_ref, core, base_ref),
        (near_ref, other(core), near_base_ref),
    ):
        out_ref[0] = (
            raw_ref[which].astype(f32) + near_raw_ref[which].astype(f32)
        ).astype(bf16)
        out_ref[1] = base[0]


def merge(raw, near_raw, base, near_base):
    shape = pltpu.HBM(raw.shape, bf16)
    return pl.pallas_call(
        merge_kernel,
        out_shape=(shape, shape),
        cost_estimate=estimate(10 * base.size),
        compiler_params=compiler_params(),
        name="merge",
    )(raw, near_raw, base, near_base)


def send_kernel(
    replicas, own_ref, away_ref, got_ref, got_away_ref, params_ref, momentum_ref, out_ref
):
    out_ref[0] = (away_ref[0, 0].astype(f32) + got_away_ref[0].astype(f32)).astype(bf16)
    summed = own_ref[0, 0].astype(f32) + got_ref[0].astype(f32)
    out_ref[1] = based(replicas, params_ref[...], momentum_ref[...], summed)


def send_part(replicas, delta, got, params, momentum, start, width):
    _, _, rows, _ = delta.shape
    step = step_of(start, width)
    return pl.pallas_call(
        functools.partial(send_kernel, replicas),
        grid=(width // step,),
        in_specs=[
            slab_spec(rows, step, start, False, False),
            slab_spec(rows, step, start, True, False),
            got_spec(rows, step, False),
            got_spec(rows, step, True),
            state_spec(rows, step, start),
            state_spec(rows, step, start),
        ],
        out_specs=pl.BlockSpec((2, rows, step * lane), lambda i: (0, 0, i)),
        out_shape=pltpu.HBM((2, rows, width * lane), bf16),
        cost_estimate=estimate(20 * rows * width * lane),
        compiler_params=compiler_params(),
        name="send_part",
    )(delta, delta, got, got, params, momentum)


def finish_kernel(replicas, own, near, *refs):
    outs = refs[-(2 * own + 1) :]
    working_ref = outs[-1]
    if own:
        (
            own_ref, got_ref, params_ref, momentum_ref,
            sent_sum, sent_base, far_sum, far_base,
        ) = refs[:8]
        refs = refs[8:]
        summed = own_ref[0, 0].astype(f32) + got_ref[0].astype(f32)
        average = (summed + far_sum[0].astype(f32)) * (1 / replicas)
        momentum_new = nesterov_keep * momentum_ref[...] + average
        outs[1][...] = momentum_new
        outs[0][...] = params_ref[...] - outer_rate * (
            average + nesterov_keep * momentum_new
        )
        chip, core = slab(False, False)
        core = core if near else 0
        working_ref[chip, core] = joined(replicas, sent_base[0], far_sum[0])
        working_ref[other(chip), core] = joined(replicas, far_base[0], sent_sum[0])
    if near:
        sent_sum, sent_base, far_sum, far_base = refs[:4]
        chip, core = slab(False, True) if own else (slab(False, False)[0], 0)
        working_ref[chip, core] = joined(replicas, sent_base[0], far_sum[0])
        working_ref[other(chip), core] = joined(replicas, far_base[0], sent_sum[0])


def finish(replicas, part, got, sent, far, near_sent, near_far, results, after, own, near):
    delta, params, momentum, start, width = part
    chips, cores_, rows, columns = delta.shape
    step = step_of(start, width)
    state = state_spec(rows, step, start)
    state_shape = jax.ShapeDtypeStruct((rows, columns), f32)
    operands, in_specs = [], []
    if own:
        operands += [delta, got, params, momentum]
        in_specs += [
            slab_spec(rows, step, start, False, False),
            got_spec(rows, step, False),
            state,
            state,
        ]
    for wanted, pair in ((own, sent), (own, far), (near, near_sent), (near, near_far)):
        if wanted:
            operands += [pair, pair]
            in_specs += [half_spec(rows, step, 0), half_spec(rows, step, 1)]
    for array in after:
        operands.append(array)
        in_specs.append(any_spec())
    aliases = {}
    if results is not None:
        for i, array in enumerate(results if own else results[-1:]):
            aliases[len(operands)] = i
            operands.append(array)
            in_specs.append(any_spec())
    both = own and near
    count = cores_ if both else 1
    working_spec = pl.BlockSpec(
        (chips, count, rows, step * lane),
        lambda i: (0, 0 if both else slab(False, near)[1], 0, start // step + i),
    )
    working_shape = jax.ShapeDtypeStruct(delta.shape, bf16)
    outs = pl.pallas_call(
        functools.partial(finish_kernel, replicas, own, near),
        grid=(width // step,),
        in_specs=in_specs,
        out_specs=(state, state, working_spec) if own else (working_spec,),
        out_shape=(state_shape, state_shape, working_shape) if own else (working_shape,),
        input_output_aliases=aliases,
        cost_estimate=estimate((32 * own + 12 * near) * rows * width * lane),
        compiler_params=compiler_params(),
        name="finish",
    )(*operands)
    return tuple(outs) if own else (*results[:-1], outs[0])


def local(enc_delta, enc_params, enc_momentum, dec_delta, dec_params, dec_momentum):
    replicas = lax.axis_size("replica")
    near = [(r, r + 1 - 2 * (r % 2)) for r in range(replicas)]
    far = [(r, (r + replicas // 2) % replicas) for r in range(replicas)]

    def swap(x, pairs):
        return lax.ppermute(x, "replica", pairs)

    parts = []
    for block, (deltas, params, momentum, shares) in enumerate((
        (enc_delta, enc_params, enc_momentum, first_shares),
        (dec_delta, dec_params, dec_momentum, last_shares),
    )):
        _, _, rows, columns = params.shape
        delta = deltas.reshape(2, replicas // 2, rows, columns)
        params = params.reshape(rows, columns)
        momentum = momentum.reshape(rows, columns)
        chunks = chunks_of(columns, shares)
        if block == 0:
            chunks.append(chunks.pop(raw_share))
        for start, width in chunks:
            parts.append((block, (delta, params, momentum, start, width)))

    raw_at = len(first_shares) - 1
    raw_part = parts[raw_at][1]
    gots, sents, fars, near_sents = [], [], [], []
    for i, (_, part) in enumerate(parts):
        delta, params, momentum, start, width = part
        if i == 0:
            picked, raw = open_part(delta, start, width, *raw_part[3:])
        else:
            behind = [picked] if i == 2 else [sents[i - 1]]
            picked = pick(delta, start, width, behind)
        got = swap(picked, near)
        if i == 0:
            far_raw = swap(raw, far)
        sent = send_part(replicas, delta, got, params, momentum, start, width)
        out = sent
        if i == raw_at:
            out = sent[1:]
        came = swap(out, far)
        near_sent = swap(sent, near)
        gots.append(got)
        sents.append(sent)
        fars.append(came)
        near_sents.append(near_sent)

    arrays = [None, None]
    after = [sents[-1]]
    for i, (block, part) in enumerate(parts):
        came = fars[i]
        near_came = swap(came, near)
        if i == raw_at:
            near_raw = swap(far_raw, near)
            came, near_came = merge(far_raw, near_raw, came, near_came)
        last = i == len(parts) - 1
        inputs = (gots[i], sents[i], came, near_sents[i], near_came)
        arrays[block] = finish(
            replicas, part, *inputs, arrays[block], after, True, not last
        )
        if last:
            arrays[block] = finish(
                replicas, part, *inputs, arrays[block], [], False, True
            )
        after = []

    results = []
    for params_new, momentum_new, working in arrays:
        rows, columns = params_new.shape
        results.append(
            (
                params_new.reshape(1, 1, rows, columns),
                momentum_new.reshape(1, 1, rows, columns),
                working.reshape(replicas * rows, columns),
            )
        )
    return (*results[0], *results[1])


def solution(mesh):
    delta_spec = P("replica", "shard", None)
    state = P("replica", "shard", None, None)
    return jax.shard_map(
        local,
        mesh=mesh,
        in_specs=(delta_spec, state, state, delta_spec, state, state),
        out_specs=(state, state, P("shard", None), state, state, P("shard", None)),
        check_vma=False,
    )
```

```python
import functools

import jax
import jax.numpy as jnp
from jax import lax
from jax.experimental import pallas as pl
from jax.experimental.pallas import tpu as pltpu
from jax.sharding import PartitionSpec as P


outer_rate = 0.7
nesterov_keep = 0.9
lane = 128
widest = 8
vmem_bytes = 67_043_328

first_shares = (4, 2, 2, 8, 16, 32)
raw_share = 1
last_shares = (3, 1, 4, 8, 16, 32)
last_order = (5, 1, 4, 3, 2, 0)

f32 = jnp.float32
bf16 = jnp.bfloat16


def chunks_of(columns, shares):
    units = columns // lane
    total = sum(shares)
    edges, seen = [0], 0
    for share in shares:
        seen += share
        edges.append(max(edges[-1], units * seen // total))
    return [(a, b - a) for a, b in zip(edges[:-1], edges[1:]) if b > a]


def step_of(start, width):
    for units in (widest, 4, 3, 2, 1):
        if start % units == 0 and width % units == 0:
            return units
    return 1


def cores():
    return lax.axis_size("replica") // 2


def chip_core():
    r = lax.axis_index("replica")
    return r // cores(), lax.rem(r, cores())


def other(i):
    return 1 - i


def slab(far, near):
    chip, core = chip_core()
    return (other(chip) if far else chip), (other(core) if near else core)


def slab_spec(rows, step, start, far, near):
    return pl.BlockSpec(
        (1, 1, rows, step * lane),
        lambda i: (*slab(far, near), 0, start // step + i),
    )


def got_spec(rows, step, far):
    return pl.BlockSpec(
        (1, rows, step * lane), lambda i: (slab(far, False)[0], 0, i)
    )


def state_spec(rows, step, start):
    return pl.BlockSpec((rows, step * lane), lambda i: (0, start // step + i))


def half_spec(rows, step, half):
    return pl.BlockSpec((1, rows, step * lane), lambda i: (half, 0, i))


def any_spec():
    return pl.BlockSpec(memory_space=pl.ANY)


def estimate(bytes_moved):
    return pl.CostEstimate(
        flops=bytes_moved, bytes_accessed=bytes_moved, transcendentals=0
    )


def compiler_params():
    return pltpu.CompilerParams(vmem_limit_bytes=vmem_bytes)


def share(replicas):
    return outer_rate * (1 + nesterov_keep) / replicas


def based(replicas, params, momentum, summed):
    kept = params - (outer_rate * nesterov_keep**2) * momentum
    return (kept - share(replicas) * summed).astype(bf16)


def joined(replicas, base, summed):
    return (base.astype(f32) - share(replicas) * summed.astype(f32)).astype(bf16)


def pick_kernel(in_ref, *refs):
    refs[-1][...] = in_ref[:, 0]


def pick(delta, start, width, after):
    chips, _, rows, _ = delta.shape
    step = step_of(start, width)
    return pl.pallas_call(
        pick_kernel,
        grid=(width // step,),
        in_specs=[
            pl.BlockSpec(
                (chips, 1, rows, step * lane),
                lambda i: (0, slab(False, True)[1], 0, start // step + i),
            )
        ]
        + [any_spec()] * len(after),
        out_specs=pl.BlockSpec((chips, rows, step * lane), lambda i: (0, 0, i)),
        out_shape=pltpu.HBM((chips, rows, width * lane), bf16),
        cost_estimate=estimate(8 * rows * width * lane),
        compiler_params=compiler_params(),
        name="pick",
    )(delta, *after)


def open_kernel(near_ref, far_ref, picked_ref, raw_ref):
    picked_ref[...] = near_ref[:, 0]
    raw_ref[...] = far_ref[0]


def open_part(delta, start, width, raw_start, raw_width):
    chips, cores_, rows, _ = delta.shape
    return pl.pallas_call(
        open_kernel,
        grid=(1,),
        in_specs=[
            pl.BlockSpec(
                (chips, 1, rows, width * lane),
                lambda i: (0, slab(False, True)[1], 0, start // width),
            ),
            pl.BlockSpec(
                (1, cores_, rows, raw_width * lane),
                lambda i: (slab(True, False)[0], 0, 0, raw_start // raw_width),
            ),
        ],
        out_specs=(
            pl.BlockSpec((chips, rows, width * lane), lambda i: (0, 0, 0)),
            pl.BlockSpec((cores_, rows, raw_width * lane), lambda i: (0, 0, 0)),
        ),
        out_shape=(
            pltpu.HBM((chips, rows, width * lane), bf16),
            pltpu.HBM((cores_, rows, raw_width * lane), bf16),
        ),
        cost_estimate=estimate(8 * rows * (width + raw_width) * lane),
        compiler_params=compiler_params(),
        name="open_part",
    )(delta, delta)


def merge_kernel(raw_ref, near_raw_ref, base_ref, near_base_ref, far_ref, near_ref):
    core = slab(False, False)[1]
    for out_ref, which, base in (
        (far_ref, core, base_ref),
        (near_ref, other(core), near_base_ref),
    ):
        out_ref[0] = (
            raw_ref[which].astype(f32) + near_raw_ref[which].astype(f32)
        ).astype(bf16)
        out_ref[1] = base[0]


def merge(raw, near_raw, base, near_base):
    shape = pltpu.HBM(raw.shape, bf16)
    return pl.pallas_call(
        merge_kernel,
        out_shape=(shape, shape),
        cost_estimate=estimate(10 * base.size),
        compiler_params=compiler_params(),
        name="merge",
    )(raw, near_raw, base, near_base)


def send_kernel(
    replicas, own_ref, away_ref, got_ref, got_away_ref, params_ref, momentum_ref, out_ref
):
    out_ref[0] = (away_ref[0, 0].astype(f32) + got_away_ref[0].astype(f32)).astype(bf16)
    summed = own_ref[0, 0].astype(f32) + got_ref[0].astype(f32)
    out_ref[1] = based(replicas, params_ref[...], momentum_ref[...], summed)


def send_part(replicas, delta, got, params, momentum, start, width):
    _, _, rows, _ = delta.shape
    step = step_of(start, width)
    return pl.pallas_call(
        functools.partial(send_kernel, replicas),
        grid=(width // step,),
        in_specs=[
            slab_spec(rows, step, start, False, False),
            slab_spec(rows, step, start, True, False),
            got_spec(rows, step, False),
            got_spec(rows, step, True),
            state_spec(rows, step, start),
            state_spec(rows, step, start),
        ],
        out_specs=pl.BlockSpec((2, rows, step * lane), lambda i: (0, 0, i)),
        out_shape=pltpu.HBM((2, rows, width * lane), bf16),
        cost_estimate=estimate(20 * rows * width * lane),
        compiler_params=compiler_params(),
        name="send_part",
    )(delta, delta, got, got, params, momentum)


def finish_kernel(replicas, own, near, *refs):
    outs = refs[-(2 * own + 1) :]
    working_ref = outs[-1]
    if own:
        (
            own_ref, got_ref, params_ref, momentum_ref,
            sent_sum, sent_base, far_sum, far_base,
        ) = refs[:8]
        refs = refs[8:]
        summed = own_ref[0, 0].astype(f32) + got_ref[0].astype(f32)
        average = (summed + far_sum[0].astype(f32)) * (1 / replicas)
        momentum_new = nesterov_keep * momentum_ref[...] + average
        outs[1][...] = momentum_new
        outs[0][...] = params_ref[...] - outer_rate * (
            average + nesterov_keep * momentum_new
        )
        chip, core = slab(False, False)
        core = core if near else 0
        working_ref[chip, core] = joined(replicas, sent_base[0], far_sum[0])
        working_ref[other(chip), core] = joined(replicas, far_base[0], sent_sum[0])
    if near:
        sent_sum, sent_base, far_sum, far_base = refs[:4]
        chip, core = slab(False, True) if own else (slab(False, False)[0], 0)
        working_ref[chip, core] = joined(replicas, sent_base[0], far_sum[0])
        working_ref[other(chip), core] = joined(replicas, far_base[0], sent_sum[0])


def finish(replicas, part, got, sent, far, near_sent, near_far, results, after, own, near):
    delta, params, momentum, start, width = part
    chips, cores_, rows, columns = delta.shape
    step = step_of(start, width)
    state = state_spec(rows, step, start)
    state_shape = jax.ShapeDtypeStruct((rows, columns), f32)
    operands, in_specs = [], []
    if own:
        operands += [delta, got, params, momentum]
        in_specs += [
            slab_spec(rows, step, start, False, False),
            got_spec(rows, step, False),
            state,
            state,
        ]
    for wanted, pair in ((own, sent), (own, far), (near, near_sent), (near, near_far)):
        if wanted:
            operands += [pair, pair]
            in_specs += [half_spec(rows, step, 0), half_spec(rows, step, 1)]
    for array in after:
        operands.append(array)
        in_specs.append(any_spec())
    aliases = {}
    if results is not None:
        for i, array in enumerate(results if own else results[-1:]):
            aliases[len(operands)] = i
            operands.append(array)
            in_specs.append(any_spec())
    both = own and near
    count = cores_ if both else 1
    working_spec = pl.BlockSpec(
        (chips, count, rows, step * lane),
        lambda i: (0, 0 if both else slab(False, near)[1], 0, start // step + i),
    )
    working_shape = jax.ShapeDtypeStruct(delta.shape, bf16)
    outs = pl.pallas_call(
        functools.partial(finish_kernel, replicas, own, near),
        grid=(width // step,),
        in_specs=in_specs,
        out_specs=(state, state, working_spec) if own else (working_spec,),
        out_shape=(state_shape, state_shape, working_shape) if own else (working_shape,),
        input_output_aliases=aliases,
        cost_estimate=estimate((32 * own + 12 * near) * rows * width * lane),
        compiler_params=compiler_params(),
        name="finish",
    )(*operands)
    return tuple(outs) if own else (*results[:-1], outs[0])


def local(enc_delta, enc_params, enc_momentum, dec_delta, dec_params, dec_momentum):
    replicas = lax.axis_size("replica")
    near = [(r, r + 1 - 2 * (r % 2)) for r in range(replicas)]
    far = [(r, (r + replicas // 2) % replicas) for r in range(replicas)]

    def swap(x, pairs):
        return lax.ppermute(x, "replica", pairs)

    parts = []
    for block, (deltas, params, momentum, shares) in enumerate((
        (enc_delta, enc_params, enc_momentum, first_shares),
        (dec_delta, dec_params, dec_momentum, last_shares),
    )):
        _, _, rows, columns = params.shape
        delta = deltas.reshape(2, replicas // 2, rows, columns)
        params = params.reshape(rows, columns)
        momentum = momentum.reshape(rows, columns)
        chunks = chunks_of(columns, shares)
        if block == 0:
            chunks.append(chunks.pop(raw_share))
        else:
            chunks = [chunks[i] for i in last_order]
        for start, width in chunks:
            parts.append((block, (delta, params, momentum, start, width)))

    raw_at = len(first_shares) - 1
    raw_part = parts[raw_at][1]
    gots, sents, fars, near_sents = [], [], [], []
    for i, (_, part) in enumerate(parts):
        delta, params, momentum, start, width = part
        if i == 0:
            picked, raw = open_part(delta, start, width, *raw_part[3:])
        else:
            behind = [picked] if i == 2 else [sents[i - 1]]
            picked = pick(delta, start, width, behind)
        got = swap(picked, near)
        if i == 0:
            far_raw = swap(raw, far)
        sent = send_part(replicas, delta, got, params, momentum, start, width)
        out = sent
        if i == raw_at:
            out = sent[1:]
        came = swap(out, far)
        near_sent = swap(sent, near)
        gots.append(got)
        sents.append(sent)
        fars.append(came)
        near_sents.append(near_sent)

    arrays = [None, None]
    after = [sents[-1]]
    for i, (block, part) in enumerate(parts):
        came = fars[i]
        near_came = swap(came, near)
        if i == raw_at:
            near_raw = swap(far_raw, near)
            came, near_came = merge(far_raw, near_raw, came, near_came)
        last = i == len(parts) - 1
        inputs = (gots[i], sents[i], came, near_sents[i], near_came)
        arrays[block] = finish(
            replicas, part, *inputs, arrays[block], after, True, not last
        )
        if last:
            arrays[block] = finish(
                replicas, part, *inputs, arrays[block], [], False, True
            )
        after = []

    results = []
    for params_new, momentum_new, working in arrays:
        rows, columns = params_new.shape
        results.append(
            (
                params_new.reshape(1, 1, rows, columns),
                momentum_new.reshape(1, 1, rows, columns),
                working.reshape(replicas * rows, columns),
            )
        )
    return (*results[0], *results[1])


def solution(mesh):
    delta_spec = P("replica", "shard", None)
    state = P("replica", "shard", None, None)
    return jax.shard_map(
        local,
        mesh=mesh,
        in_specs=(delta_spec, state, state, delta_spec, state, state),
        out_specs=(state, state, P("shard", None), state, state, P("shard", None)),
        check_vma=False,
    )
```
